768 devices in a mesh: dp: 192 (over z, y, core), seq: 4 (over x).
Axes of the slice: x: 4, y: 8, z: 12, core: 2. Of those that a mesh axis runs over, the one named last changes fastest.
Arguments:
- queries: bfloat16 [192, 512, 2048], P('dp', 'seq'), may hold values from -6 to 6
- keys: bfloat16 [192, 512, 2048], P('dp', 'seq'), may hold values from -6 to 6
- values: bfloat16 [192, 512, 2048], P('dp', 'seq'), may hold values from -6 to 6
- decay_bias: float32 [192, 16, 512], P('dp', None, 'seq'), may hold values from -14 to -1
- gate_matrix: bfloat16 [6144, 16], replicated, may hold values from -0.078125 to 0.078125
- resets: int32 [192, 4], P('dp', 'seq'), may hold values 0 or 1
- cotangent: bfloat16 [192, 512, 2048], P('dp', 'seq'), may hold values from -6 to 6
Outputs:
- output: bfloat16 [192, 512, 2048], P('dp', 'seq')
- grad_queries: bfloat16 [192, 512, 2048], P('dp', 'seq')
- grad_keys: bfloat16 [192, 512, 2048], P('dp', 'seq')
- grad_values: bfloat16 [192, 512, 2048], P('dp', 'seq')
- grad_gate: float32 [6144, 16], P(('dp', 'seq'))
The draws below stay inside these ranges and needn't reach their ends.
All inputs are finite; a program needn't handle non-finite values. No bound on the sum of `resets` on one device may be relied on, other than what follows from the above.
Results may differ from the reference program's by a relative error of at most 0.012.
Values may be sent and summed in bfloat16 or wider, within the bound.
A program may use at most 64 MiB of HBM per device.

```python
import jax
import jax.numpy as jnp
from jax import lax

HEADS = 16
HEAD_DIM = 128
BLOCK = 128
TOK_DEV = 128
PACKED_TOTAL = 192
WINDOW_TOKENS = 512
BLOCKS = 4
WIDTH = 2048
GATE_IN = 6144


def draw_decay_bias(key, part):
    pick_key = jax.random.fold_in(key, 11)
    slow_key = jax.random.fold_in(key, 12)
    quick_key = jax.random.fold_in(key, 13)
    shift_key = jax.random.fold_in(key, 14)
    spike_prng_seed = jax.random.fold_in(key, 15)
    fast_share = 0.5
    chosen = jax.random.uniform(pick_key, (PACKED_TOTAL, HEADS, 1)) < fast_share
    gradual_frequencies = jnp.log(jax.random.uniform(slow_key, (PACKED_TOTAL, HEADS, 1), minval=0.05, maxval=0.4) / WINDOW_TOKENS) - 0.5
    quick_rates = jnp.log(jax.random.uniform(quick_key, (PACKED_TOTAL, HEADS, 1), minval=1.0 / 50.0, maxval=1.0 / 30.0)) - 0.5
    default_frequencies = jnp.where(chosen, quick_rates, gradual_frequencies)
    portion_shift = jax.random.uniform(shift_key, (PACKED_TOTAL, 1, WINDOW_TOKENS // TOK_DEV), minval=-0.7, maxval=0.7)
    portion_shift = jnp.repeat(portion_shift, TOK_DEV, axis=2)
    spike_occurrences = jax.random.bernoulli(spike_prng_seed, 3.0 / WINDOW_TOKENS, (PACKED_TOTAL, 1, WINDOW_TOKENS))
    return jnp.where(spike_occurrences, -1.2, default_frequencies + portion_shift).astype(jnp.float32)


def place_ends(array, rng, smallest, top_value):
    dims = array.shape
    spot = [jax.random.randint(jax.random.fold_in(rng, axis), (), 0, dims[axis]) for axis in range(len(dims))]
    array = array.at[tuple(spot)].set(smallest)
    longest = dims.index(max(dims))
    spot[longest] = (spot[longest] + 1) % dims[longest]
    return array.at[tuple(spot)].set(top_value)


def block_levels(own_key, extent, cuts, least, largest):
    level, own = 1.0, jax.random.fold_in(own_key, 6)
    for position, blocks in cuts:
        draws = jnp.exp(jax.random.uniform(jax.random.fold_in(own, position), (blocks,), jnp.float32, least / len(cuts), largest / len(cuts)))
        level = level * jnp.repeat(draws, extent[position] // blocks).reshape([-1 if axis == position else 1 for axis in range(len(extent))])
    return level


def noise(key, extent, scale, most, shards=(), kind=jnp.bfloat16):
    loudness = block_levels(key, extent, shards, -0.22, 0.18) if shards else 1.0
    result = jax.random.normal(key, extent, jnp.float32) * scale * loudness
    return jnp.minimum(jnp.maximum(result, -most), most).astype(kind)


def setup_inputs(seed: int = 0) -> dict:
    splits = jax.random.split(jax.random.key(seed), 8)
    queries = noise(splits[0], (PACKED_TOTAL, WINDOW_TOKENS, WIDTH), 1.0, 6.0, ((0, 192), (1, 4)))
    keys = noise(splits[1], (PACKED_TOTAL, WINDOW_TOKENS, WIDTH), 1.0, 6.0, ((0, 192), (1, 4)))
    values = noise(splits[2], (PACKED_TOTAL, WINDOW_TOKENS, WIDTH), 1.0, 6.0, ((0, 192), (1, 4)))
    decay_bias = draw_decay_bias(jax.random.fold_in(splits[7], 71), 0)
    gate_matrix = noise(splits[4], (GATE_IN, HEADS), GATE_IN ** -0.5, 0.078125)
    resets = place_ends((jax.random.randint(splits[5], (PACKED_TOTAL, BLOCKS), 0, 3) < 1).astype(jnp.int32), jax.random.fold_in(splits[5], 1), 0, 1)
    cotangent = noise(splits[6], (PACKED_TOTAL, WINDOW_TOKENS, WIDTH), 1.0, 6.0, ((0, 192), (1, 4)))
    return dict(queries=queries, keys=keys, values=values, decay_bias=decay_bias, gate_matrix=gate_matrix, resets=resets, cotangent=cotangent)


EPSILON = 1e-06

def one_sequence(queries, keys, values, bias_rows, resets, cotangent, gate_matrix):
    model_width = HEADS * HEAD_DIM
    shape_four = (BLOCKS, BLOCK, HEADS, HEAD_DIM)
    query_blocks = queries.reshape(shape_four).astype(jnp.float32)
    key_blocks = keys.reshape(shape_four).astype(jnp.float32)
    value_blocks = values.reshape(shape_four).astype(jnp.float32)
    joined = jnp.concatenate([queries, keys, values], axis=1)
    logits = jnp.dot(joined, gate_matrix, preferred_element_type=jnp.float32) + bias_rows.T
    logdecay = -jax.nn.softplus(logits)
    cumulative = jnp.cumsum(logdecay.reshape(BLOCKS, BLOCK, HEADS), axis=1)
    totals = cumulative[:, -1, :]
    kept_flags = (1 - resets).astype(jnp.float32)
    factors = kept_flags[:, None] * jnp.exp(totals)
    fading = jnp.exp(totals[:, None, :] - cumulative)
    decayed_keys = (fading[..., None] * key_blocks).astype(jnp.bfloat16)
    updates = jnp.einsum('nche,nchf->nhef', decayed_keys.astype(jnp.float32), value_blocks)

    def advance(carried_state, element):
        factor_row, flag_row, update_row = element
        return (factor_row[:, None, None] * carried_state + update_row, flag_row * carried_state)
    zero_state = jnp.zeros((HEADS, HEAD_DIM, HEAD_DIM), jnp.float32)
    _, entering = lax.scan(advance, zero_state, (factors, kept_flags, updates))
    ending = jnp.exp(totals)[:, :, None, None] * entering + updates
    scores = jnp.einsum('nthe,nshe->nhts', query_blocks, key_blocks)
    cum_heads = jnp.transpose(cumulative, (0, 2, 1))
    lower_mask = jnp.tril(jnp.ones((BLOCK, BLOCK), dtype=bool))
    differences = cum_heads[:, :, :, None] - cum_heads[:, :, None, :]
    decays = jnp.exp(jnp.where(lower_mask, differences, -jnp.inf))
    attn = decays * scores
    attn_b = attn.astype(jnp.bfloat16)
    within = jnp.einsum('nhts,nshf->nthf', attn_b.astype(jnp.float32), value_blocks)
    entering_b = entering.astype(jnp.bfloat16)
    carried = jnp.exp(cumulative)[..., None] * jnp.einsum('nthe,nhef->nthf', query_blocks, entering_b.astype(jnp.float32))
    mixture = within + carried
    norm_root = jnp.sqrt(lax.optimization_barrier(jnp.mean(mixture * mixture, axis=-1, keepdims=True)) + EPSILON)
    normed = mixture / norm_root
    output = normed.astype(jnp.bfloat16).reshape(WINDOW_TOKENS, model_width)
    upstream = cotangent.reshape(shape_four).astype(jnp.float32)
    d_mixture = (upstream - normed * lax.optimization_barrier(jnp.mean(upstream * normed, axis=-1, keepdims=True))) / norm_root
    d_mixture_b = d_mixture.astype(jnp.bfloat16)
    d_mix_wide = d_mixture_b.astype(jnp.float32)
    d_attn = jnp.einsum('nthf,nshf->nhts', d_mix_wide, value_blocks)
    weighted = (decays * d_attn).astype(jnp.bfloat16).astype(jnp.float32)
    q_decay = (jnp.exp(cumulative)[..., None] * query_blocks).astype(jnp.bfloat16)
    local_grad = jnp.einsum('nthe,nthf->nhef', q_decay.astype(jnp.float32), d_mix_wide)
    pushed = kept_flags[:, None, None, None] * local_grad

    def retreat(carried_grad, element):
        factor_row, pushed_row = element
        return (factor_row[:, None, None] * carried_grad + pushed_row, carried_grad)
    _, state_grads = lax.scan(retreat, zero_state, (factors, pushed), reverse=True)
    state_grads_b = state_grads.astype(jnp.bfloat16).astype(jnp.float32)
    from_state = fading[..., None] * jnp.einsum('nthf,nhef->nthe', value_blocks, state_grads_b)
    products = attn * d_attn
    d_cumul = jnp.transpose(lax.optimization_barrier(jnp.sum(products, axis=3)) - lax.optimization_barrier(jnp.sum(products, axis=2)), (0, 2, 1))
    d_cumul = d_cumul + lax.optimization_barrier(jnp.sum(d_mixture * carried, axis=-1)) - lax.optimization_barrier(jnp.sum(key_blocks * from_state, axis=-1))
    d_cumul = d_cumul.at[:, -1, :].add(lax.optimization_barrier(jnp.sum(state_grads * ending, axis=(2, 3))))
    d_logdecay = jnp.cumsum(d_cumul[:, ::-1, :], axis=1)[:, ::-1, :]
    d_logits = (-jax.nn.sigmoid(logits) * d_logdecay.reshape(WINDOW_TOKENS, HEADS)).astype(jnp.bfloat16)
    gate_back = jnp.dot(d_logits, gate_matrix.T, preferred_element_type=jnp.float32)
    grad_q = jnp.einsum('nhts,nshe->nthe', weighted, key_blocks)
    grad_q = grad_q + jnp.exp(cumulative)[..., None] * jnp.einsum('nthf,nhef->nthe', d_mix_wide, entering_b.astype(jnp.float32))
    grad_k = jnp.einsum('nhts,nthe->nshe', weighted, query_blocks) + from_state
    grad_v = jnp.einsum('nhts,nthf->nshf', attn_b.astype(jnp.float32), d_mix_wide)
    grad_v = grad_v + fading[..., None] * jnp.einsum('nthe,nhef->nthf', key_blocks, state_grads_b)
    grad_q = (grad_q.reshape(WINDOW_TOKENS, model_width) + gate_back[:, :model_width]).astype(jnp.bfloat16)
    grad_k = (grad_k.reshape(WINDOW_TOKENS, model_width) + gate_back[:, model_width:2 * model_width]).astype(jnp.bfloat16)
    grad_v = (grad_v.reshape(WINDOW_TOKENS, model_width) + gate_back[:, 2 * model_width:]).astype(jnp.bfloat16)
    weight_term = jnp.dot(joined.T, d_logits, preferred_element_type=jnp.float32)
    return (output, grad_q, grad_k, grad_v, weight_term)

def reference(queries, keys, values, decay_bias, gate_matrix, resets, cotangent):

    def per_sequence(accumulated, element):
        question_vectors, key_rows, value_rows, bias_rows, reset_row, cot_rows = element
        output, grad_q, grad_k, grad_v, weight_term = one_sequence(question_vectors, key_rows, value_rows, bias_rows, reset_row, cot_rows, gate_matrix)
        return (accumulated + weight_term, (output, grad_q, grad_k, grad_v))
    starting_sum = jnp.zeros((GATE_IN, HEADS), jnp.float32)
    grad_gate, (output, grad_q, grad_k, grad_v) = lax.scan(per_sequence, starting_sum, (queries, keys, values, decay_bias, resets, cotangent))
    return (output, grad_q, grad_k, grad_v, grad_gate)
```

```python
import functools

import jax
import jax.numpy as jnp
from jax import lax
from jax.experimental import pallas as pl
from jax.experimental.pallas import tpu as pltpu
from jax.sharding import PartitionSpec as P

EPSILON = 1e-06
HEADS = 16
D = 128
NX, NY, NZ, NC = 4, 8, 12, 2
MESH = pl.DeviceIdType.MESH
F32 = jnp.float32
BF16 = jnp.bfloat16
STATE, GRAD, TERM = BF16, BF16, BF16
GROUP = 2
KERNEL_VMEM = 40 * 1024 * 1024
LAG = 5


def nn(a, b):
    return jnp.dot(a, b, preferred_element_type=F32)


def nt(a, b):
    return lax.dot_general(a, b, (((1,), (1,)), ((), ())), preferred_element_type=F32)


def tn(a, b):
    return lax.dot_general(a, b, (((0,), (0,)), ((), ())), preferred_element_type=F32)


def exact(a, b):
    return jnp.dot(a, b, preferred_element_type=F32, precision=lax.Precision.HIGHEST)


def kernel(
    reset_ref, q_hbm, k_hbm, v_hbm, bias_hbm, gt_hbm, ct_hbm,
    out_ref, gq_ref, gk_ref, gv_ref, gg_ref,
    q_ref, k_ref, v_ref, bias_ref, gt_ref, ct_ref, in_sem,
    cum, sig, dcum, wl,
    e_s, fad_s, upd, ending, lgrad, qacc, kacc, vacc, zacc,
    e_in, e_out, g_in, g_out, jt,
    m1, r1, x_out, r2, t3, r3, y4, r4,
    fs_sem, fr_sem, bs_sem, br_sem,
    s1s, s1r, s2s, s2r, s3s, s3r, s4s, s4r,
):
    loads = [
        pltpu.make_async_copy(src, dst, in_sem.at[i])
        for i, (src, dst) in enumerate((
            (gt_hbm, gt_ref), (q_hbm, q_ref), (k_hbm, k_ref), (v_hbm, v_ref), (bias_hbm, bias_ref), (ct_hbm, ct_ref)
        ))
    ]
    for load in loads:
        load.start()

    c = lax.axis_index("seq")
    dp = lax.axis_index("dp")
    core = lax.rem(dp, NC)
    y = lax.rem(lax.div(dp, NC), NY)
    z = lax.div(dp, NC * NY)

    def dp_of(zz, yy, cc):
        return (zz * NY + yy) * NC + cc

    partner = dp_of(z, y, 1 - core)
    x_peers = [lax.rem(c + d, NX) for d in range(1, NX)]
    z_peers = [lax.rem(z + d, NZ) for d in range(1, NZ)]
    y_peers = [lax.rem(y + d, NY) for d in range(1, NY)]

    barrier = pltpu.get_barrier_semaphore()

    def greet(device):
        pl.semaphore_signal(barrier, inc=1, device_id=device, device_id_type=MESH)

    for peer in x_peers:
        greet({"seq": peer})
    greet({"dp": partner})
    for peer in z_peers:
        greet({"dp": dp_of(peer, y, core)})
    for peer in y_peers:
        greet({"dp": dp_of(z, peer, core)})

    def remote(src, dst, send, recv, device):
        return pltpu.make_async_remote_copy(
            src_ref=src, dst_ref=dst, send_sem=send, recv_sem=recv,
            device_id=device, device_id_type=MESH,
        )

    def fwd_copy(h):
        return remote(e_out.at[h], e_in.at[h], fs_sem.at[h], fr_sem.at[h], {"seq": lax.rem(c + 1, NX)})

    def bwd_copy(h):
        return remote(g_out.at[h], g_in.at[h], bs_sem.at[h], br_sem.at[h], {"seq": lax.rem(c + NX - 1, NX)})

    first, last = c == 0, c == NX - 1
    kept = (1 - reset_ref[0, 0]).astype(F32)
    rows = lax.broadcasted_iota(jnp.int32, (D, D), 0)
    lanes = lax.broadcasted_iota(jnp.int32, (D, D), 1)

    def cols(ref, h):
        return ref[0, :, pl.ds(pl.multiple_of(h * D, D), D)]

    w = HEADS * D
    logits = None
    loads[0].wait()
    for i, ref in enumerate((q_ref, k_ref, v_ref)):
        loads[i + 1].wait()
        term = nt(ref[0], gt_ref[:, i * w : (i + 1) * w])
        logits = term if logits is None else logits + term
    loads[4].wait()
    logits = logits.T + bias_ref[0]
    logdecay = -(jnp.maximum(logits, 0.0) + jnp.log1p(jnp.exp(-jnp.abs(logits))))
    sig[...] = 1.0 / (1.0 + jnp.exp(-logits))
    cum[...] = exact(logdecay, (rows <= lanes).astype(F32))

    loads[5].wait()
    pl.semaphore_wait(barrier, NX - 1 + 1 + NZ - 1 + NY - 1)

    def updates(p, carry):
        hs = [p * 4 + i for i in range(4)]
        col = [jnp.broadcast_to(cum[pl.ds(h, 1), :], (D, D)).T for h in hs]
        key = [cols(k_ref, h).astype(F32) for h in hs]
        val = [cols(v_ref, h) for h in hs]
        fad = [jnp.exp(x[D - 1 : D, :] - x) for x in col]
        e = [jnp.exp(x) for x in col]
        u = [tn((f * k).astype(BF16), v) for f, k, v in zip(fad, key, val)]
        for i, h in enumerate(hs):
            e_s[h] = e[i]
            fad_s[h] = fad[i]
            upd[h] = u[i]

        @pl.when(first)
        def _():
            for i, h in enumerate(hs):
                e_out[h] = u[i].astype(STATE)
            for h in hs:
                e_in[h] = jnp.zeros((D, D), STATE)
            for h in hs:
                fwd_copy(h).start()

        @pl.when(last)
        def _():
            for h in hs:
                g_in[h] = jnp.zeros((D, D), GRAD)

        return carry

    lax.fori_loop(0, HEADS // 4, updates, 0)

    def forward(hs):
        for h in hs:

            @pl.when(jnp.logical_not(first))
            def _():
                fwd_copy(h).wait_recv()

            @pl.when(jnp.logical_not(first) & jnp.logical_not(last))
            def _():
                e_out[h] = (e_s[h, D - 1 : D, :] * (kept * e_in[h].astype(F32)) + upd[h]).astype(STATE)
                fwd_copy(h).start()

        entering = [kept * e_in[h].astype(F32) for h in hs]
        end = [e_s[h, D - 1 : D, :] * x + upd[h] for h, x in zip(hs, entering)]
        q = [cols(q_ref, h) for h in hs]
        k = [cols(k_ref, h) for h in hs]
        v = [cols(v_ref, h) for h in hs]
        up = [cols(ct_ref, h).astype(F32) for h in hs]
        e = [e_s[h] for h in hs]
        row = [jnp.broadcast_to(cum[pl.ds(h, 1), :], (D, D)) for h in hs]
        e_b = [x.astype(BF16) for x in entering]
        scores = [nt(a, b) for a, b in zip(q, k)]
        reach = [nn(a, b) for a, b in zip(q, e_b)]
        dec = [jnp.exp(jnp.where(rows >= lanes, x.T - x, -1e30)) for x in row]
        attn = [a * b for a, b in zip(dec, scores)]
        attn_b = [x.astype(BF16) for x in attn]
        within = [nn(a, b) for a, b in zip(attn_b, v)]
        carried = [a * b for a, b in zip(e, reach)]
        mixture = [a + b for a, b in zip(within, carried)]
        root = [jnp.sqrt(jnp.mean(x * x, axis=1, keepdims=True) + EPSILON) for x in mixture]
        normed = [a / b for a, b in zip(mixture, root)]
        dm = [(u - x * jnp.mean(u * x, axis=1, keepdims=True)) / r for u, x, r in zip(up, normed, root)]
        dm_b = [x.astype(BF16) for x in dm]
        qd = [(a * b.astype(F32)).astype(BF16) for a, b in zip(e, q)]
        local = [kept * tn(a, b) for a, b in zip(qd, dm_b)]
        da = [nt(a, b) for a, b in zip(dm_b, v)]
        gq = [nt(a, b) for a, b in zip(dm_b, e_b)]
        gv = [tn(a, b) for a, b in zip(attn_b, dm_b)]
        prod = [a * b for a, b in zip(attn, da)]
        wt = [(a * b).astype(BF16) for a, b in zip(dec, da)]
        gq = [nn(a, b) + c0 * d for a, b, c0, d in zip(wt, k, e, gq)]
        gk = [tn(a, b) for a, b in zip(wt, q)]
        turned = [[piece.T for piece in pieces] for pieces in zip(q, k, v)]
        for i, h in enumerate(hs):
            ending[h] = end[i]
            out_ref[0, :, pl.ds(pl.multiple_of(h * D, D), D)] = normed[i].astype(BF16)
            lgrad[h] = local[i]
            qacc[h] = gq[i]
            kacc[h] = gk[i]
            vacc[h] = gv[i]
            zacc[h] = prod[i] + carried[i] * dm[i]
            dcum[pl.ds(h, 1), :] = -jnp.sum(prod[i], axis=0, keepdims=True)
            for j in range(3):
                jt[pl.ds(pl.multiple_of(j * w + h * D, D), D), :] = turned[i][j]

    def backward(hs):
        for h in hs:

            @pl.when(jnp.logical_not(last))
            def _():
                bwd_copy(h).wait_recv()

            @pl.when(jnp.logical_not(first))
            def _():
                g_out[h] = (kept * e_s[h, D - 1 : D, :] * g_in[h].astype(F32) + lgrad[h]).astype(GRAD)
                bwd_copy(h).start()

        gf = [g_in[h].astype(F32) for h in hs]
        g = [x.astype(BF16) for x in gf]
        k = [cols(k_ref, h) for h in hs]
        v = [cols(v_ref, h) for h in hs]
        fad = [fad_s[h] for h in hs]
        fs = [f * nt(a, b) for f, a, b in zip(fad, v, g)]
        gv = [f * nn(a, b) for f, a, b in zip(fad, k, g)]
        zt = [(zacc[h] - a.astype(F32) * b).T for h, a, b in zip(hs, k, fs)]
        inner = [x * ending[h] for h, x in zip(hs, gf)]
        gk = [kacc[h] + x for h, x in zip(hs, fs)]
        gv = [vacc[h] + x for h, x in zip(hs, gv)]
        before = [dcum[pl.ds(h, 1), :] for h in hs]
        for i, h in enumerate(hs):
            kacc[h] = gk[i]
            vacc[h] = gv[i]
            dcum[pl.ds(h, 1), :] = before[i] + jnp.sum(zt[i], axis=0, keepdims=True)
            wl[pl.ds(h, 1), :] = jnp.sum(inner[i], axis=0, keepdims=True)

    steps = HEADS // GROUP
    lag = jnp.where(last, 0, jnp.where(c == NX - 2, LAG, steps))

    def step(j, carry):
        @pl.when(j < steps)
        def _():
            forward([j * GROUP + i for i in range(GROUP)])

        @pl.when(j >= lag)
        def _():
            backward([(j - lag) * GROUP + i for i in range(GROUP)])

        return carry

    lax.fori_loop(0, steps + lag, step, 0)

    at_end = jnp.where(
        lax.broadcasted_iota(jnp.int32, (HEADS, D), 1) == D - 1, jnp.sum(wl[...], axis=1, keepdims=True), 0.0
    )
    d_logdecay = exact(dcum[...] + at_end, (rows >= lanes).astype(F32))
    dl = (-sig[...] * d_logdecay).astype(BF16)

    dl8 = jnp.concatenate([dl] * NY, axis=0)
    group = lax.div(lax.broadcasted_iota(jnp.int32, (NC * NX * 8, D), 1), HEADS)

    def gate_rows(zz, carry):
        r = nt(jt[pl.ds(pl.multiple_of(zz * 512, 512), 512), :], dl8)
        acc = r[:64]
        for yy in range(1, NY):
            acc = jnp.where(group == yy, r[yy * 64 : (yy + 1) * 64], acc)
        for cc in range(NC):
            for xx in range(NX):
                at = (cc * NX + xx) * 8
                m1[cc, xx, zz] = acc[at : at + 8]
        return carry

    lax.fori_loop(0, NZ, gate_rows, 0, unroll=3)

    copy1 = remote(m1.at[1 - core], r1, s1s, s1r, {"dp": partner})
    copy1.start()

    def finish(acc, ref, part):
        def one(h, carry):
            back = tn(dl, gt_ref[:, pl.ds(pl.multiple_of(part * w + h * D, D), D)])
            ref[0, :, pl.ds(pl.multiple_of(h * D, D), D)] = (acc[h] + back).astype(BF16)
            return carry

        lax.fori_loop(0, HEADS, one, 0, unroll=4)

    copy1.wait()

    for xx in range(NX):
        t3[xx] = m1[core, xx] + r1[xx]
        x_out[xx] = t3[xx].reshape(NZ * 8, D).astype(TERM)
    copies2 = []
    for d in (2, 1, 3):
        peer = x_peers[d - 1]
        copies2.append(remote(x_out.at[peer], r2.at[d - 1], s2s.at[d - 1], s2r.at[d - 1], {"seq": peer}))
        copies2[-1].start()
    finish(qacc, gq_ref, 0)
    for copy in copies2:
        copy.wait()

    total = t3[c].reshape(NZ * 8, D) + r2[0].astype(F32) + r2[1].astype(F32) + r2[2].astype(F32)
    z_out = t3.at[c]
    z_out[...] = total.reshape(NZ, 8, D)
    copies3 = []
    for d in (6, 5, 7, 4, 8, 3, 9, 2, 10, 1, 11):
        peer = z_peers[d - 1]
        copies3.append(
            remote(z_out.at[peer], r3.at[d - 1], s3s.at[d - 1], s3r.at[d - 1], {"dp": dp_of(peer, y, core)})
        )
        copies3[-1].start()
    finish(kacc, gk_ref, 1)
    finish(vacc, gv_ref, 2)
    for copy in copies3:
        copy.wait()

    tile = t3[c, z]
    for d in range(NZ - 1):
        tile = tile + r3[d]
    y4[...] = tile
    copies4 = []
    for d in (4, 3, 5, 2, 6, 1, 7):
        peer = y_peers[d - 1]
        copies4.append(remote(y4, r4.at[d - 1], s4s.at[d - 1], s4r.at[d - 1], {"dp": dp_of(z, peer, core)}))
        copies4[-1].start()
    for copy in copies4:
        copy.wait()
    for d in range(NY - 1):
        tile = tile + r4[d]
    mine = tile[:, :HEADS]
    for yy in range(1, NY):
        mine = jnp.where(y == yy, tile[:, yy * HEADS : (yy + 1) * HEADS], mine)
    gg_ref[...] = mine

    def drain(h, carry):
        @pl.when(jnp.logical_not(last))
        def _():
            fwd_copy(h).wait_send()

        @pl.when(jnp.logical_not(first))
        def _():
            bwd_copy(h).wait_send()

        return carry

    lax.fori_loop(0, HEADS, drain, 0)


def put_out(*refs):
    sem = refs[10]
    copies = [pltpu.make_async_copy(refs[i], refs[5 + i], sem.at[i]) for i in range(5)]
    for copy in copies:
        copy.start()
    for copy in copies:
        copy.wait()


def body(queries, keys, values, decay_bias, gate_matrix, resets, cotangent):
    vmem = pl.BlockSpec(memory_space=pltpu.VMEM)
    smem = pl.BlockSpec(memory_space=pltpu.SMEM)
    states = (HEADS, D, D)
    big = pltpu.VMEM(states, F32)
    dma = pltpu.SemaphoreType.DMA
    small = pltpu.VMEM((HEADS, D), F32)
    rows = jax.ShapeDtypeStruct((1, D, HEADS * D), BF16)
    hbm = pl.BlockSpec(memory_space=pltpu.HBM)
    small_out = jax.ShapeDtypeStruct((8, HEADS), F32)
    tokens = pltpu.VMEM((1, D, HEADS * D), BF16)
    args = (queries, keys, values, decay_bias, gate_matrix.T, cotangent)
    results = pl.pallas_call(
        kernel,
        name="gated_attention",
        out_shape=(rows, rows, rows, rows, small_out),
        in_specs=[smem] + [hbm] * 6,
        out_specs=[vmem] * 5,
        scratch_shapes=[
            tokens, tokens, tokens, pltpu.VMEM((1, HEADS, D), F32), pltpu.VMEM((HEADS, 3 * HEADS * D), BF16), tokens, dma((6,)),
            small, small, small, small,
            big, big, big, big, big, big, big, big, big,
            pltpu.VMEM(states, STATE), pltpu.VMEM(states, STATE), pltpu.VMEM(states, GRAD), pltpu.VMEM(states, GRAD),
            pltpu.VMEM((3 * HEADS * D, D), BF16),
            pltpu.VMEM((NC, NX, NZ, 8, D), F32),
            pltpu.VMEM((NX, NZ, 8, D), F32),
            pltpu.VMEM((NX, NZ * 8, D), TERM),
            pltpu.VMEM((NX - 1, NZ * 8, D), TERM),
            pltpu.VMEM((NX, NZ, 8, D), F32),
            pltpu.VMEM((NZ - 1, 8, D), F32),
            pltpu.VMEM((8, D), F32),
            pltpu.VMEM((NY - 1, 8, D), F32),
            dma((HEADS,)), dma((HEADS,)), dma((HEADS,)), dma((HEADS,)),
            dma, dma, dma((NX - 1,)), dma((NX - 1,)),
            dma((NZ - 1,)), dma((NZ - 1,)), dma((NY - 1,)), dma((NY - 1,)),
        ],
        compiler_params=pltpu.CompilerParams(
            collective_id=0, has_side_effects=True, vmem_limit_bytes=KERNEL_VMEM
        ),
    )(resets, *[pltpu.with_memory_space_constraint(x, pltpu.HBM) for x in args])
    return pl.pallas_call(
        put_out,
        name="put_out",
        out_shape=(rows, rows, rows, rows, small_out),
        in_specs=[vmem] * 5,
        out_specs=[hbm] * 5,
        scratch_shapes=[dma((5,))],
        compiler_params=pltpu.CompilerParams(vmem_limit_bytes=1024 * 1024),
    )(*results)


def solution(mesh):
    tokens = P("dp", "seq", None)
    return jax.shard_map(
        body,
        mesh=mesh,
        in_specs=(tokens, tokens, tokens, P("dp", None, "seq"), P(), P("dp", "seq"), tokens),
        out_specs=(tokens, tokens, tokens, tokens, P(("dp", "seq"), None)),
        check_vma=False,
    )
```

```python
import functools

import jax
import jax.numpy as jnp
from jax import lax
from jax.experimental import pallas as pl
from jax.experimental.pallas import tpu as pltpu
from jax.sharding import PartitionSpec as P

EPSILON = 1e-06
HEADS = 16
D = 128
NX, NY, NZ, NC = 4, 8, 12, 2
MESH = pl.DeviceIdType.MESH
F32 = jnp.float32
BF16 = jnp.bfloat16
STATE, GRAD, TERM = BF16, BF16, BF16
GROUP = 2
KERNEL_VMEM = 40 * 1024 * 1024
LAG = 4


def nn(a, b):
    return jnp.dot(a, b, preferred_element_type=F32)


def nt(a, b):
    return lax.dot_general(a, b, (((1,), (1,)), ((), ())), preferred_element_type=F32)


def tn(a, b):
    return lax.dot_general(a, b, (((0,), (0,)), ((), ())), preferred_element_type=F32)


def exact(a, b):
    return jnp.dot(a, b, preferred_element_type=F32, precision=lax.Precision.HIGHEST)


def kernel(
    reset_ref, q_hbm, k_hbm, v_hbm, bias_hbm, gt_hbm, ct_hbm,
    out_ref, gq_ref, gk_ref, gv_ref, gg_ref,
    q_ref, k_ref, v_ref, bias_ref, gt_ref, ct_ref, in_sem,
    cum, sig, dcum, wl,
    e_s, fad_s, upd, ending, lgrad, qacc, kacc, vacc, zacc,
    e_in, e_out, g_in, g_out, jt,
    m1, r1, x_out, r2, t3, r3, y4, r4,
    fs_sem, fr_sem, bs_sem, br_sem,
    s1s, s1r, s2s, s2r, s3s, s3r, s4s, s4r,
):
    loads = [
        pltpu.make_async_copy(src, dst, in_sem.at[i])
        for i, (src, dst) in enumerate((
            (gt_hbm, gt_ref), (q_hbm, q_ref), (k_hbm, k_ref), (v_hbm, v_ref), (bias_hbm, bias_ref), (ct_hbm, ct_ref)
        ))
    ]
    for load in loads:
        load.start()

    c = lax.axis_index("seq")
    dp = lax.axis_index("dp")
    core = lax.rem(dp, NC)
    y = lax.rem(lax.div(dp, NC), NY)
    z = lax.div(dp, NC * NY)

    def dp_of(zz, yy, cc):
        return (zz * NY + yy) * NC + cc

    partner = dp_of(z, y, 1 - core)
    x_peers = [lax.rem(c + d, NX) for d in range(1, NX)]
    z_peers = [lax.rem(z + d, NZ) for d in range(1, NZ)]
    y_peers = [lax.rem(y + d, NY) for d in range(1, NY)]

    barrier = pltpu.get_barrier_semaphore()

    def greet(device):
        pl.semaphore_signal(barrier, inc=1, device_id=device, device_id_type=MESH)

    for peer in x_peers:
        greet({"seq": peer})
    greet({"dp": partner})
    for peer in z_peers:
        greet({"dp": dp_of(peer, y, core)})
    for peer in y_peers:
        greet({"dp": dp_of(z, peer, core)})

    def remote(src, dst, send, recv, device):
        return pltpu.make_async_remote_copy(
            src_ref=src, dst_ref=dst, send_sem=send, recv_sem=recv,
            device_id=device, device_id_type=MESH,
        )

    def fwd_copy(h):
        return remote(e_out.at[h], e_in.at[h], fs_sem.at[h], fr_sem.at[h], {"seq": lax.rem(c + 1, NX)})

    def bwd_copy(h):
        return remote(g_out.at[h], g_in.at[h], bs_sem.at[h], br_sem.at[h], {"seq": lax.rem(c + NX - 1, NX)})

    first, last = c == 0, c == NX - 1
    kept = (1 - reset_ref[0, 0]).astype(F32)
    rows = lax.broadcasted_iota(jnp.int32, (D, D), 0)
    lanes = lax.broadcasted_iota(jnp.int32, (D, D), 1)

    def cols(ref, h):
        return ref[0, :, pl.ds(pl.multiple_of(h * D, D), D)]

    w = HEADS * D
    logits = None
    loads[0].wait()
    for i, ref in enumerate((q_ref, k_ref, v_ref)):
        loads[i + 1].wait()
        term = nt(ref[0], gt_ref[:, i * w : (i + 1) * w])
        logits = term if logits is None else logits + term
    loads[4].wait()
    logits = logits.T + bias_ref[0]
    logdecay = -(jnp.maximum(logits, 0.0) + jnp.log1p(jnp.exp(-jnp.abs(logits))))
    sig[...] = 1.0 / (1.0 + jnp.exp(-logits))
    cum[...] = exact(logdecay, (rows <= lanes).astype(F32))

    loads[5].wait()
    pl.semaphore_wait(barrier, NX - 1 + 1 + NZ - 1 + NY - 1)

    def updates(p, carry):
        hs = [p * 4 + i for i in range(4)]
        col = [jnp.broadcast_to(cum[pl.ds(h, 1), :], (D, D)).T for h in hs]
        key = [cols(k_ref, h).astype(F32) for h in hs]
        val = [cols(v_ref, h) for h in hs]
        fad = [jnp.exp(x[D - 1 : D, :] - x) for x in col]
        e = [jnp.exp(x) for x in col]
        u = [tn((f * k).astype(BF16), v) for f, k, v in zip(fad, key, val)]
        for i, h in enumerate(hs):
            e_s[h] = e[i]
            fad_s[h] = fad[i]
            upd[h] = u[i]

        @pl.when(first)
        def _():
            for i, h in enumerate(hs):
                e_out[h] = u[i].astype(STATE)
            for h in hs:
                e_in[h] = jnp.zeros((D, D), STATE)
            for h in hs:
                fwd_copy(h).start()

        @pl.when(last)
        def _():
            for h in hs:
                g_in[h] = jnp.zeros((D, D), GRAD)

        return carry

    lax.fori_loop(0, HEADS // 4, updates, 0)

    def forward(hs):
        for h in hs:

            @pl.when(jnp.logical_not(first))
            def _():
                fwd_copy(h).wait_recv()

            @pl.when(jnp.logical_not(first) & jnp.logical_not(last))
            def _():
                e_out[h] = (e_s[h, D - 1 : D, :] * (kept * e_in[h].astype(F32)) + upd[h]).astype(STATE)
                fwd_copy(h).start()

        entering = [kept * e_in[h].astype(F32) for h in hs]
        end = [e_s[h, D - 1 : D, :] * x + upd[h] for h, x in zip(hs, entering)]
        q = [cols(q_ref, h) for h in hs]
        k = [cols(k_ref, h) for h in hs]
        v = [cols(v_ref, h) for h in hs]
        up = [cols(ct_ref, h).astype(F32) for h in hs]
        e = [e_s[h] for h in hs]
        row = [jnp.broadcast_to(cum[pl.ds(h, 1), :], (D, D)) for h in hs]
        e_b = [x.astype(BF16) for x in entering]
        scores = [nt(a, b) for a, b in zip(q, k)]
        reach = [nn(a, b) for a, b in zip(q, e_b)]
        dec = [jnp.exp(jnp.where(rows >= lanes, x.T - x, -1e30)) for x in row]
        attn = [a * b for a, b in zip(dec, scores)]
        attn_b = [x.astype(BF16) for x in attn]
        within = [nn(a, b) for a, b in zip(attn_b, v)]
        carried = [a * b for a, b in zip(e, reach)]
        mixture = [a + b for a, b in zip(within, carried)]
        root = [jnp.sqrt(jnp.mean(x * x, axis=1, keepdims=True) + EPSILON) for x in mixture]
        normed = [a / b for a, b in zip(mixture, root)]
        dm = [(u - x * jnp.mean(u * x, axis=1, keepdims=True)) / r for u, x, r in zip(up, normed, root)]
        dm_b = [x.astype(BF16) for x in dm]
        qd = [(a * b.astype(F32)).astype(BF16) for a, b in zip(e, q)]
        local = [kept * tn(a, b) for a, b in zip(qd, dm_b)]
        da = [nt(a, b) for a, b in zip(dm_b, v)]
        gq = [nt(a, b) for a, b in zip(dm_b, e_b)]
        gv = [tn(a, b) for a, b in zip(attn_b, dm_b)]
        prod = [a * b for a, b in zip(attn, da)]
        wt = [(a * b).astype(BF16) for a, b in zip(dec, da)]
        gq = [nn(a, b) + c0 * d for a, b, c0, d in zip(wt, k, e, gq)]
        gk = [tn(a, b) for a, b in zip(wt, q)]
        turned = [[piece.T for piece in pieces] for pieces in zip(q, k, v)]
        for i, h in enumerate(hs):
            ending[h] = end[i]
            out_ref[0, :, pl.ds(pl.multiple_of(h * D, D), D)] = normed[i].astype(BF16)
            lgrad[h] = local[i]
            qacc[h] = gq[i]
            kacc[h] = gk[i]
            vacc[h] = gv[i]
            zacc[h] = prod[i] + carried[i] * dm[i]
            dcum[pl.ds(h, 1), :] = -jnp.sum(prod[i], axis=0, keepdims=True)
            for j in range(3):
                jt[pl.ds(pl.multiple_of(j * w + h * D, D), D), :] = turned[i][j]

    def backward(hs):
        for h in hs:

            @pl.when(jnp.logical_not(last))
            def _():
                bwd_copy(h).wait_recv()

            @pl.when(jnp.logical_not(first))
            def _():
                g_out[h] = (kept * e_s[h, D - 1 : D, :] * g_in[h].astype(F32) + lgrad[h]).astype(GRAD)
                bwd_copy(h).start()

        gf = [g_in[h].astype(F32) for h in hs]
        g = [x.astype(BF16) for x in gf]
        k = [cols(k_ref, h) for h in hs]
        v = [cols(v_ref, h) for h in hs]
        fad = [fad_s[h] for h in hs]
        fs = [f * nt(a, b) for f, a, b in zip(fad, v, g)]
        gv = [f * nn(a, b) for f, a, b in zip(fad, k, g)]
        zt = [(zacc[h] - a.astype(F32) * b).T for h, a, b in zip(hs, k, fs)]
        inner = [x * ending[h] for h, x in zip(hs, gf)]
        gk = [kacc[h] + x for h, x in zip(hs, fs)]
        gv = [vacc[h] + x for h, x in zip(hs, gv)]
        before = [dcum[pl.ds(h, 1), :] for h in hs]
        for i, h in enumerate(hs):
            kacc[h] = gk[i]
            vacc[h] = gv[i]
            dcum[pl.ds(h, 1), :] = before[i] + jnp.sum(zt[i], axis=0, keepdims=True)
            wl[pl.ds(h, 1), :] = jnp.sum(inner[i], axis=0, keepdims=True)

    steps = HEADS // GROUP
    lag = jnp.where(last, 0, jnp.where(c == NX - 2, LAG, steps))

    def step(j, carry):
        @pl.when(j < steps)
        def _():
            forward([j * GROUP + i for i in range(GROUP)])

        @pl.when(j >= lag)
        def _():
            backward([(j - lag) * GROUP + i for i in range(GROUP)])

        return carry

    lax.fori_loop(0, steps + lag, step, 0)

    at_end = jnp.where(
        lax.broadcasted_iota(jnp.int32, (HEADS, D), 1) == D - 1, jnp.sum(wl[...], axis=1, keepdims=True), 0.0
    )
    d_logdecay = exact(dcum[...] + at_end, (rows >= lanes).astype(F32))
    dl = (-sig[...] * d_logdecay).astype(BF16)

    dl8 = jnp.concatenate([dl] * NY, axis=0)
    group = lax.div(lax.broadcasted_iota(jnp.int32, (NC * NX * 8, D), 1), HEADS)

    def gate_rows(zz, carry):
        r = nt(jt[pl.ds(pl.multiple_of(zz * 512, 512), 512), :], dl8)
        acc = r[:64]
        for yy in range(1, NY):
            acc = jnp.where(group == yy, r[yy * 64 : (yy + 1) * 64], acc)
        for cc in range(NC):
            for xx in range(NX):
                at = (cc * NX + xx) * 8
                m1[cc, xx, zz] = acc[at : at + 8]
        return carry

    lax.fori_loop(0, NZ, gate_rows, 0, unroll=3)

    copy1 = remote(m1.at[1 - core], r1, s1s, s1r, {"dp": partner})
    copy1.start()

    def finish(acc, ref, part):
        def one(h, carry):
            back = tn(dl, gt_ref[:, pl.ds(pl.multiple_of(part * w + h * D, D), D)])
            ref[0, :, pl.ds(pl.multiple_of(h * D, D), D)] = (acc[h] + back).astype(BF16)
            return carry

        lax.fori_loop(0, HEADS, one, 0, unroll=4)

    copy1.wait()

    for xx in range(NX):
        t3[xx] = m1[core, xx] + r1[xx]
        x_out[xx] = t3[xx].reshape(NZ * 8, D).astype(TERM)
    copies2 = []
    for d in (2, 1, 3):
        peer = x_peers[d - 1]
        copies2.append(remote(x_out.at[peer], r2.at[d - 1], s2s.at[d - 1], s2r.at[d - 1], {"seq": peer}))
        copies2[-1].start()
    finish(qacc, gq_ref, 0)
    for copy in copies2:
        copy.wait()

    total = t3[c].reshape(NZ * 8, D) + r2[0].astype(F32) + r2[1].astype(F32) + r2[2].astype(F32)
    z_out = t3.at[c]
    z_out[...] = total.reshape(NZ, 8, D)
    copies3 = []
    for d in (6, 5, 7, 4, 8, 3, 9, 2, 10, 1, 11):
        peer = z_peers[d - 1]
        copies3.append(
            remote(z_out.at[peer], r3.at[d - 1], s3s.at[d - 1], s3r.at[d - 1], {"dp": dp_of(peer, y, core)})
        )
        copies3[-1].start()
    finish(kacc, gk_ref, 1)
    finish(vacc, gv_ref, 2)
    for copy in copies3:
        copy.wait()

    tile = t3[c, z]
    for d in range(NZ - 1):
        tile = tile + r3[d]
    y4[...] = tile
    copies4 = []
    for d in (4, 3, 5, 2, 6, 1, 7):
        peer = y_peers[d - 1]
        copies4.append(remote(y4, r4.at[d - 1], s4s.at[d - 1], s4r.at[d - 1], {"dp": dp_of(z, peer, core)}))
        copies4[-1].start()
    for copy in copies4:
        copy.wait()
    for d in range(NY - 1):
        tile = tile + r4[d]
    mine = tile[:, :HEADS]
    for yy in range(1, NY):
        mine = jnp.where(y == yy, tile[:, yy * HEADS : (yy + 1) * HEADS], mine)
    gg_ref[...] = mine

    def drain(h, carry):
        @pl.when(jnp.logical_not(last))
        def _():
            fwd_copy(h).wait_send()

        @pl.when(jnp.logical_not(first))
        def _():
            bwd_copy(h).wait_send()

        return carry

    lax.fori_loop(0, HEADS, drain, 0)


def put_out(*refs):
    sem = refs[10]
    copies = [pltpu.make_async_copy(refs[i], refs[5 + i], sem.at[i]) for i in range(5)]
    for copy in copies:
        copy.start()
    for copy in copies:
        copy.wait()


def body(queries, keys, values, decay_bias, gate_matrix, resets, cotangent):
    vmem = pl.BlockSpec(memory_space=pltpu.VMEM)
    smem = pl.BlockSpec(memory_space=pltpu.SMEM)
    states = (HEADS, D, D)
    big = pltpu.VMEM(states, F32)
    dma = pltpu.SemaphoreType.DMA
    small = pltpu.VMEM((HEADS, D), F32)
    rows = jax.ShapeDtypeStruct((1, D, HEADS * D), BF16)
    hbm = pl.BlockSpec(memory_space=pltpu.HBM)
    small_out = jax.ShapeDtypeStruct((8, HEADS), F32)
    tokens = pltpu.VMEM((1, D, HEADS * D), BF16)
    args = (queries, keys, values, decay_bias, gate_matrix.T, cotangent)
    results = pl.pallas_call(
        kernel,
        name="gated_attention",
        out_shape=(rows, rows, rows, rows, small_out),
        in_specs=[smem] + [hbm] * 6,
        out_specs=[vmem] * 5,
        scratch_shapes=[
            tokens, tokens, tokens, pltpu.VMEM((1, HEADS, D), F32), pltpu.VMEM((HEADS, 3 * HEADS * D), BF16), tokens, dma((6,)),
            small, small, small, small,
            big, big, big, big, big, big, big, big, big,
            pltpu.VMEM(states, STATE), pltpu.VMEM(states, STATE), pltpu.VMEM(states, GRAD), pltpu.VMEM(states, GRAD),
            pltpu.VMEM((3 * HEADS * D, D), BF16),
            pltpu.VMEM((NC, NX, NZ, 8, D), F32),
            pltpu.VMEM((NX, NZ, 8, D), F32),
            pltpu.VMEM((NX, NZ * 8, D), TERM),
            pltpu.VMEM((NX - 1, NZ * 8, D), TERM),
            pltpu.VMEM((NX, NZ, 8, D), F32),
            pltpu.VMEM((NZ - 1, 8, D), F32),
            pltpu.VMEM((8, D), F32),
            pltpu.VMEM((NY - 1, 8, D), F32),
            dma((HEADS,)), dma((HEADS,)), dma((HEADS,)), dma((HEADS,)),
            dma, dma, dma((NX - 1,)), dma((NX - 1,)),
            dma((NZ - 1,)), dma((NZ - 1,)), dma((NY - 1,)), dma((NY - 1,)),
        ],
        compiler_params=pltpu.CompilerParams(
            collective_id=0, has_side_effects=True, vmem_limit_bytes=KERNEL_VMEM
        ),
    )(resets, *[pltpu.with_memory_space_constraint(x, pltpu.HBM) for x in args])
    return pl.pallas_call(
        put_out,
        name="put_out",
        out_shape=(rows, rows, rows, rows, small_out),
        in_specs=[vmem] * 5,
        out_specs=[hbm] * 5,
        scratch_shapes=[dma((5,))],
        compiler_params=pltpu.CompilerParams(vmem_limit_bytes=1024 * 1024),
    )(*results)


def solution(mesh):
    tokens = P("dp", "seq", None)
    return jax.shard_map(
        body,
        mesh=mesh,
        in_specs=(tokens, tokens, tokens, P("dp", None, "seq"), P(), P("dp", "seq"), tokens),
        out_specs=(tokens, tokens, tokens, tokens, P(("dp", "seq"), None)),
        check_vma=False,
    )
```
